32 devices in a mesh: tm: 16 (over z, y, x), body: 2 (over core).
Axes of the slice: x: 2, y: 2, z: 4, core: 2. Of those that a mesh axis runs over, the one named last changes fastest.
Arguments:
- states: float32 [16, 6, 2048], P('tm', None, 'body'), may hold values from -3 to 3, as said below
- masses: float32 [2048], P('body'), may hold values from 0.25 to 4
- frequency: float32 [2048], P('body'), may hold values from 0.35 to 1
Outputs:
- fine_end: float32 [16, 6, 2048], P('tm', None, 'body')
- correction: float32 [16, 6, 2048], P('tm', None, 'body')
- next_start: float32 [16, 6, 2048], P('tm', None, 'body')
The draws below stay inside these ranges and needn't reach their ends.
Inputs may be any that keep to these rules, and one draw needn't show every extreme that they name: `states`: each body's distance from the z axis lies between 1 and 2 and its |z| is at most 0.2 in every slice's state.
All inputs are finite; a program needn't handle non-finite values.
Results may differ from the reference program's by a relative error of at most 0.0001.
Values sent between devices are 32-bit elements; how exact they have to be, the bound alone decides.
A program may use at most 64 MiB of HBM per device.

```python
import math
import jax
import jax.numpy as jnp
from jax import lax

BODIES = 2048
SLICES = 16


def guiding_radius(key):
    radius = jax.random.uniform(jax.random.fold_in(key, 3), (BODIES,), jnp.float32, 1.0, 2.0)
    return radius


def draw_frequency(key, part):
    radius = guiding_radius(key)
    return (radius ** (-1.5)).astype(jnp.float32)


def circular_speed(radius):
    return 1.0 / jnp.sqrt(radius)


def draw_states(key, part):
    keys = jax.random.split(jax.random.fold_in(key, 7), 12)
    shape = (SLICES, BODIES)
    guide = guiding_radius(key)[None, :]
    angles = jax.random.uniform(keys[1], shape, jnp.float32, -jnp.pi, jnp.pi)
    spread = jnp.clip(0.02 * jax.random.normal(keys[0], shape, jnp.float32), -0.06, 0.06)
    height = jnp.clip(0.05 * jax.random.normal(keys[2], shape, jnp.float32), -0.2, 0.2)
    radial = jnp.clip(0.05 * jax.random.normal(keys[3], shape, jnp.float32), -0.2, 0.2)
    vertical = jnp.clip(0.05 * jax.random.normal(keys[4], shape, jnp.float32), -0.2, 0.2)
    excess = jnp.clip(0.05 * jax.random.normal(keys[5], shape, jnp.float32), -0.2, 0.2)
    radius = jnp.clip(guide * (1.0 + spread), 1.0, 2.0)
    circular = circular_speed(radius) * (1.0 + excess)
    cos_angle = jnp.cos(angles)
    sin_angle = jnp.sin(angles)
    disc_state = jnp.stack([radius * cos_angle, radius * sin_angle, height, radial * cos_angle - circular * sin_angle, radial * sin_angle + circular * cos_angle, vertical], axis=1)
    centre_angle = jax.random.uniform(keys[6], (SLICES, 1), jnp.float32, -jnp.pi, jnp.pi)
    clump_gap = 0.7
    centre_radius = 1.5
    member_draw = jax.random.uniform(keys[7], shape, jnp.float32, 0.0, 1.0)
    in_first = member_draw < 0.2
    in_second = jnp.logical_and(member_draw >= 0.2, member_draw < 0.4)
    in_clump = jnp.logical_or(in_first, in_second)
    first_x = centre_radius * jnp.cos(centre_angle)
    first_y = centre_radius * jnp.sin(centre_angle)
    second_x = centre_radius * jnp.cos(centre_angle + clump_gap)
    second_y = centre_radius * jnp.sin(centre_angle + clump_gap)
    chord = jnp.sqrt((second_x - first_x) ** 2 + (second_y - first_y) ** 2)
    toward_x = (second_x - first_x) / chord
    toward_y = (second_y - first_y) / chord
    clump_angle = centre_angle + jnp.where(in_second, clump_gap, 0.0)
    stream_sign = jnp.where(in_second, -1.0, 1.0)
    reach = 0.3 * jnp.sqrt(jax.random.uniform(keys[8], shape, jnp.float32, 0.0, 1.0))
    turn = jax.random.uniform(keys[9], shape, jnp.float32, -jnp.pi, jnp.pi)
    offset_x = reach * jnp.cos(turn)
    offset_y = reach * jnp.sin(turn)
    clump_height = jnp.clip(0.05 * jax.random.normal(keys[10], shape, jnp.float32), -0.15, 0.15)
    jitter = jnp.clip(0.05 * jax.random.normal(keys[11], (3, SLICES, BODIES), jnp.float32), -0.1, 0.1)
    stream_speed = 1.5
    orbit = circular_speed(centre_radius)
    clump_x = centre_radius * jnp.cos(clump_angle) + offset_x
    clump_y = centre_radius * jnp.sin(clump_angle) + offset_y
    clump_vx = -orbit * jnp.sin(clump_angle) + stream_sign * stream_speed * toward_x + jitter[0]
    clump_vy = orbit * jnp.cos(clump_angle) + stream_sign * stream_speed * toward_y + jitter[1]
    clump_state = jnp.stack([clump_x, clump_y, clump_height, clump_vx, clump_vy, jitter[2]], axis=1)
    combined = jnp.where(in_clump[:, None, :], clump_state, disc_state)
    return combined.astype(jnp.float32)


def level_of(own_key, dims, cuts, low, high):
    gain = 1.0
    for axis_at, parts in cuts:
        steps = jax.random.uniform(jax.random.fold_in(jax.random.fold_in(own_key, 6), axis_at), (parts,), jnp.float32, low / len(cuts), high / len(cuts))
        gain = gain * jnp.repeat(jnp.exp(steps), dims[axis_at] // parts).reshape((-1,) + (1,) * (len(dims) - 1 - axis_at))
    return gain


def setup_inputs(seed: int = 0) -> dict:
    arg_keys = jax.random.split(jax.random.key(seed), 4)
    return {
        "states": draw_states(jax.random.fold_in(arg_keys[3], 71), 0),
        "masses": jnp.clip(jnp.exp(math.log(4.0) - 2.7725887 * jax.random.uniform(arg_keys[1], (BODIES,), jnp.float32) ** level_of(arg_keys[1], (BODIES,), ((0, 2),), -0.2, 0.2)), 0.25, 4.0),
        "frequency": draw_frequency(jax.random.fold_in(arg_keys[3], 71), 0),
    }


slice_time = 0.25
fine_step = 0.125
soften_sq = 0.01
disc_mass = 1.0

def drift(state, count, frequency):
    angles = count * frequency * slice_time
    cos_turn = jnp.cos(angles)
    sin_turn = jnp.sin(angles)
    along_x = cos_turn * state[..., 0, :] - sin_turn * state[..., 1, :]
    along_y = sin_turn * state[..., 0, :] + cos_turn * state[..., 1, :]
    height = cos_turn * state[..., 2, :] + sin_turn * state[..., 5, :] / frequency
    speed_x = cos_turn * state[..., 3, :] - sin_turn * state[..., 4, :]
    speed_y = sin_turn * state[..., 3, :] + cos_turn * state[..., 4, :]
    speed_z = cos_turn * state[..., 5, :] - sin_turn * frequency * state[..., 2, :]
    return jnp.stack([along_x, along_y, height, speed_x, speed_y, speed_z], axis=-2)

def pair_sum(totals, source, places, speeds):
    gap_pos = source[0:3, :, None] - places[:, None, :]
    gap_vel = source[3:6, :, None] - speeds[:, None, :]
    dist_square = lax.optimization_barrier(jnp.sum(gap_pos * gap_pos, 0)) + soften_sq
    inverse = lax.rsqrt(dist_square)
    strength = source[6][:, None] * inverse * inverse * inverse
    closing = 3.0 * lax.optimization_barrier(jnp.sum(gap_pos * gap_vel, 0)) * inverse * inverse
    accels = totals[0] + lax.optimization_barrier(jnp.sum(strength[None] * gap_pos, 1))
    jerks = totals[1] + lax.optimization_barrier(jnp.sum(strength[None] * (gap_vel - closing[None] * gap_pos), 1))
    return (accels, jerks)

def scan_source(totals, source, places, speeds):
    total = source.shape[1]
    width = math.gcd(total, 512)

    def visit(turn, carry):
        block = lax.dynamic_slice_in_dim(source, turn * width, width, 1)
        return pair_sum(carry, block, places, speeds)
    return lax.fori_loop(0, total // width, visit, totals)

def star_pull(places, speeds):
    inverse = lax.rsqrt(lax.optimization_barrier(jnp.sum(places * places, 0)))
    cube = inverse * inverse * inverse
    closing = 3.0 * lax.optimization_barrier(jnp.sum(places * speeds, 0)) * inverse * inverse
    return (-cube * places, -cube * (speeds - closing * places))

def forces(places, speeds, weights):
    source = jnp.concatenate([places, speeds, weights[None, :]], 0)
    zero = jnp.zeros_like(places)
    accels, jerks = scan_source((zero, zero), source, places, speeds)
    star_acc, star_jerk = star_pull(places, speeds)
    return (accels + star_acc, jerks + star_jerk)

def hermite(state, weights):
    places, speeds = (state[0:3], state[3:6])
    accels, jerks = forces(places, speeds, weights)
    for step in range(2):
        delta = fine_step
        guess_pos = places + delta * speeds + delta * delta / 2.0 * accels + delta ** 3 / 6.0 * jerks
        guess_vel = speeds + delta * accels + delta * delta / 2.0 * jerks
        new_acc, new_jerk = forces(guess_pos, guess_vel, weights)
        new_vel = speeds + delta / 2.0 * (accels + new_acc) + delta * delta / 12.0 * (jerks - new_jerk)
        new_pos = places + delta / 2.0 * (speeds + new_vel) + delta * delta / 12.0 * (accels - new_acc)
        places, speeds, accels, jerks = (new_pos, new_vel, new_acc, new_jerk)
    return jnp.concatenate([places, speeds], 0)

def reference(states, masses, frequency):
    weights = masses * (disc_mass / BODIES)
    fine_end = lax.map(lambda state: hermite(state, weights), states)
    correction = fine_end - drift(states, 1.0, frequency)

    def advance(start, term):
        return (drift(start, 1.0, frequency) + term, start)
    _, next_start = lax.scan(advance, states[0], correction)
    return (fine_end, correction, next_start)
```

```python
import functools

import jax
import jax.numpy as jnp
from jax import lax
from jax.experimental import pallas as pl
from jax.experimental.pallas import tpu as pltpu
from jax.sharding import PartitionSpec as P

slice_time = 0.25
fine_step = 0.125
soften_sq = 0.01
disc_mass = 1.0

F32 = jnp.float32
BF16 = jnp.bfloat16
FEATURES = 48
SUM_ROWS = 16
HALF_ROWS = 8
TILE_I = 256


def group_size(count):
    best = 1
    for size in range(1, count + 1):
        if count % size == 0 and size * size <= count:
            best = size
    return best


def split3(value):
    high = value.astype(BF16).astype(F32)
    rest = value - high
    middle = rest.astype(BF16).astype(F32)
    return high, middle, rest - middle


def split2(value):
    high = value.astype(BF16).astype(F32)
    return high, value - high


def drift(planes, cos_turn, sin_turn, frequency):
    x, y, z, vx, vy, vz = planes
    return (
        cos_turn * x - sin_turn * y,
        sin_turn * x + cos_turn * y,
        cos_turn * z + sin_turn * vz / frequency,
        cos_turn * vx - sin_turn * vy,
        sin_turn * vx + cos_turn * vy,
        cos_turn * vz - sin_turn * frequency * z,
    )


def load_planes(ref):
    return tuple(ref[c] for c in range(6))


def store_planes(ref, planes):
    for c in range(6):
        ref[c] = planes[c]


def plane_sum(planes_a, planes_b):
    return sum(a * b for a, b in zip(planes_a, planes_b))


def kernel(
    nt, nb, g,
    state_hbm, mass_hbm, freq_hbm,
    out_hbm,
    state_ref, mass_ref, freq_ref, fine_ref, corr_ref, next_ref,
    feat, lhs, weigh, rhs_r, rhs_c, sum_s, sum_t,
    sendbuf, got, got_mass, grp, tot, carry_in,
    in_sem, out_sem,
    body_send, body_recv, mass_send, mass_recv,
    grp_send, grp_recv, tot_send, tot_recv, entered,
):
    slot = lax.axis_index("tm")
    half = lax.axis_index("body")
    ng = nt // g
    q = slot // g
    r = slot % g
    chunks = state_ref.shape[1]
    lanes = chunks * 128
    wide = TILE_I // 128 if chunks % (TILE_I // 128) == 0 else 1
    span = wide * 128
    touched = set()
    mass_scale = disc_mass / (lanes * nb)

    barrier = pltpu.get_barrier_semaphore()
    split = nb == 2
    later_peers = (g - 1) + (ng - 1)

    def greet_slices():
        for k in range(1, g):
            pl.semaphore_signal(barrier, inc=1, device_id={"tm": q * g + (r + k) % g})
        for k in range(1, ng):
            pl.semaphore_signal(
                barrier, inc=1, device_id={"tm": ((q + k) % ng) * g + r}
            )

    def greet():
        if split:
            @pl.when(half == 1)
            def _():
                pl.semaphore_signal(barrier, inc=1, device_id={"body": 1 - half})
        else:
            for k in range(1, nb):
                pl.semaphore_signal(barrier, inc=1, device_id={"body": (half + k) % nb})
            greet_slices()

    def meet_partner():
        if split:
            @pl.when(half == 0)
            def _():
                pl.semaphore_wait(barrier, 1)
                pl.semaphore_signal(entered.at[0], inc=1, device_id={"body": 1 - half})

            @pl.when(half == 1)
            def _():
                pl.semaphore_wait(entered.at[0], 1)
                greet_slices()
        else:
            pl.semaphore_wait(barrier, (nb - 1) + later_peers)

    def meet_slices():
        if split and later_peers:
            @pl.when(half == 1)
            def _():
                pl.semaphore_wait(barrier, later_peers)
                pl.semaphore_signal(entered.at[1], inc=1, device_id={"body": 1 - half})

            @pl.when(half == 0)
            def _():
                pl.semaphore_wait(entered.at[1], 1)

    greet()
    arrivals = [
        pltpu.make_async_copy(src, dst, in_sem.at[n])
        for n, (src, dst) in enumerate(
            ((state_hbm, state_ref), (mass_hbm, mass_ref), (freq_hbm, freq_ref))
        )
    ]
    for copy in arrivals:
        copy.start()

    def body_copy(turn, k, src):
        return pltpu.make_async_remote_copy(
            src_ref=src, dst_ref=got.at[turn, k - 1],
            send_sem=body_send.at[turn, k - 1], recv_sem=body_recv.at[turn, k - 1],
            device_id={"body": (half + k) % nb},
        )

    def mass_copy(k):
        return pltpu.make_async_remote_copy(
            src_ref=mass_ref, dst_ref=got_mass.at[k - 1],
            send_sem=mass_send.at[k - 1], recv_sem=mass_recv.at[k - 1],
            device_id={"body": (half + k) % nb},
        )

    def pieces(planes):
        split = [split3(c) for c in planes]
        norm = split3(plane_sum(planes[:3], planes[:3]))
        closing = split3(plane_sum(planes[:3], planes[3:]))
        return split, norm, closing

    one = jnp.ones((chunks, 128), F32)
    zero = jnp.zeros((chunks, 128), F32)

    def put(which, row, value):
        feat[which, :, row, :] = value

    def prepare_constants():
        for row in range(18):
            put(2, 18 + row, zero)
        for n in range(3):
            put(0, 42 + n, one)
            put(0, 45 + n, zero)
            put(2, 36 + n, one)
            put(2, 39 + n, zero)
            put(2, 45 + n, zero)
            put(3, 36 + n, zero)
            put(3, 39 + n, one)
            put(3, 45 + n, zero)
        for n in range(2):
            put(1, HALF_ROWS * n + 7, zero)

    def prepare_source(block, planes, weights, parts):
        split, norm, closing = parts
        order = (0, 0, 0, 1, 1, 2)
        for n, piece in enumerate(order):
            for c in range(6):
                put(0, 18 * (c // 3) + 3 * n + c % 3, split[c][piece])
        for n in range(3):
            put(0, 36 + n, norm[n])
            put(0, 39 + n, closing[n])
        for s in range(chunks):
            lhs[block, s * 128 : (s + 1) * 128, :] = feat[0, s].T.astype(BF16)
        heavy = [split2(weights * c) for c in planes] + [split2(weights)]
        for c in range(7):
            for n in range(2):
                put(1, HALF_ROWS * n + c, heavy[c][n])
        for s in range(chunks):
            weigh[block, :, s * 128 : (s + 1) * 128] = feat[1, s, 0:SUM_ROWS, :].astype(
                BF16
            )

    def prepare_target(parts):
        split, norm, closing = parts
        order = (0, 1, 2, 0, 1, 0)
        soft = split3(norm[0] + norm[1] + norm[2] + soften_sq)
        for n, piece in enumerate(order):
            for c in range(3):
                put(2, 3 * n + c, -2.0 * split[c][piece])
                put(3, 3 * n + c, -split[3 + c][piece])
                put(3, 18 + 3 * n + c, -split[c][piece])
        for n in range(3):
            put(2, 42 + n, soft[n])
            put(3, 42 + n, closing[n])
        for s in range(chunks):
            rhs_r[:, s * 128 : (s + 1) * 128] = feat[2, s].astype(BF16)
            rhs_c[:, s * 128 : (s + 1) * 128] = feat[3, s].astype(BF16)

    def visit(tiles):
        def pair(tile):
            block, at, n = tile
            rows = lhs[block, at * span : (at + 1) * span, :]
            cols = slice(n * span, (n + 1) * span)
            dist = jnp.dot(rows, rhs_r[:, cols], preferred_element_type=F32)
            closing = jnp.dot(rows, rhs_c[:, cols], preferred_element_type=F32)
            return dist, closing

        def curve(dist, closing):
            inverse = lax.rsqrt(dist)
            square = inverse * inverse
            strength = square * inverse
            turning = (closing * square) * strength
            s_high = strength.astype(BF16)
            s_low = (strength - s_high.astype(F32)).astype(BF16)
            return s_high, s_low, turning.astype(BF16)

        def collect(block, at, n, parts, dims):
            weights = weigh[block, :, at * span : (at + 1) * span]
            new = [
                lax.dot_general(weights, part, (dims, ((), ())), preferred_element_type=F32)
                for part in parts
            ]
            new_s, new_t = (
                a[:HALF_ROWS] + a[HALF_ROWS:] for a in (new[0] + new[1], new[2])
            )
            fresh = n not in touched
            touched.add(n)
            for m in range(wide):
                piece = slice(m * 128, (m + 1) * 128)
                if fresh:
                    sum_s[n * wide + m] = new_s[:, piece]
                    sum_t[n * wide + m] = new_t[:, piece]
                else:
                    sum_s[n * wide + m] += new_s[:, piece]
                    sum_t[n * wide + m] += new_t[:, piece]

        def gather(tile, parts):
            block, at, n = tile
            collect(block, at, n, parts, ((1,), (0,)))
            if block == 0 and at != n:
                collect(block, n, at, parts, ((1,), (1,)))

        ready, parts = pair(tiles[0]), None
        for index in range(len(tiles)):
            now = ready
            if index + 1 < len(tiles):
                ready = pair(tiles[index + 1])
            if index > 0:
                gather(tiles[index - 1], parts)
            parts = curve(*now)
        gather(tiles[-1], parts)

    def forces(turn, planes, weights, src):
        parts = pieces(planes)
        prepare_source(0, planes, weights, parts)
        prepare_target(parts)
        if turn > 0:
            for k in range(1, nb):
                body_copy(turn, k, src).start()
        touched.clear()
        squares = range(chunks // wide)
        own = [(0, at, n) for n in squares for at in squares if at >= n]
        early = 0 if split else (len(own) + 1) // 2
        if turn == 0:
            if early:
                visit(own[:early])
            meet_partner()
            for k in range(1, nb):
                body_copy(turn, k, src).start()
                mass_copy(k).start()
            visit(own[early:])
        else:
            visit(own)
        for k in range(1, nb):
            body_copy(turn, k, src).wait_recv()
            if turn == 0:
                mass_copy(k).wait_recv()
            other = load_planes(got.at[turn, k - 1])
            prepare_source(k, other, got_mass[k - 1] * mass_scale, pieces(other))
            visit([(k, at, n) for n in squares for at in squares])

        def summed(ref, c):
            return ref[:, c, :]

        places, speeds = planes[:3], planes[3:]
        total, turned = summed(sum_s, 6), summed(sum_t, 6)
        inverse = lax.rsqrt(plane_sum(places, places))
        cube = inverse * inverse * inverse
        pull = 3.0 * plane_sum(places, speeds) * inverse * inverse
        acc, jerk = [], []
        for c in range(3):
            p, v = places[c], speeds[c]
            acc.append(summed(sum_s, c) - p * total - cube * p)
            spin = summed(sum_s, 3 + c) - v * total
            spin = spin - 3.0 * (summed(sum_t, c) - p * turned)
            jerk.append(spin - cube * (v - pull * p))
        return acc, jerk

    prepare_constants()
    for copy in arrivals:
        copy.wait()
    planes = load_planes(state_ref)
    weights = mass_ref[...] * mass_scale
    h = fine_step
    acc, jerk = forces(0, planes, weights, state_ref)
    for step in range(2):
        pos, vel = planes[:3], planes[3:]
        guess = tuple(
            p + h * v + h * h / 2.0 * a + h**3 / 6.0 * j
            for p, v, a, j in zip(pos, vel, acc, jerk)
        ) + tuple(v + h * a + h * h / 2.0 * j for v, a, j in zip(vel, acc, jerk))
        out = sendbuf.at[step]
        store_planes(out, guess)
        na, nj = forces(step + 1, guess, weights, out)
        new_vel = tuple(
            vel[c] + h / 2.0 * (acc[c] + na[c]) + h * h / 12.0 * (jerk[c] - nj[c])
            for c in range(3)
        )
        new_pos = tuple(
            pos[c] + h / 2.0 * (vel[c] + new_vel[c]) + h * h / 12.0 * (acc[c] - na[c])
            for c in range(3)
        )
        planes, acc, jerk = new_pos + new_vel, na, nj
        if step == 0:
            meet_slices()

    freq = freq_ref[...]
    angle = freq * slice_time
    cos1, sin1 = jnp.cos(angle), jnp.sin(angle)
    fine = planes
    own = load_planes(state_ref)
    coarse = drift(own, cos1, sin1, freq)
    corr = tuple(a - b for a, b in zip(fine, coarse))
    first = slot == 0
    store_planes(grp.at[r], tuple(jnp.where(first, a, b) for a, b in zip(fine, corr)))
    store_planes(fine_ref, fine)
    store_planes(corr_ref, corr)

    def grp_copy(k):
        return pltpu.make_async_remote_copy(
            src_ref=grp.at[r], dst_ref=grp.at[r],
            send_sem=grp_send.at[k - 1], recv_sem=grp_recv.at[r],
            device_id={"tm": q * g + (r + k) % g},
        )

    def grp_arrival(k):
        source = (r + g - k) % g
        return pltpu.make_async_remote_copy(
            src_ref=grp.at[source], dst_ref=grp.at[source],
            send_sem=grp_send.at[k - 1], recv_sem=grp_recv.at[source],
            device_id={"tm": q * g + (r + k) % g},
        )

    for k in range(1, g):
        grp_copy(k).start()
    leaving = [
        pltpu.make_async_copy(src, out_hbm.at[n], out_sem.at[n])
        for n, src in enumerate((fine_ref, corr_ref, next_ref))
    ]
    leaving[0].start()
    leaving[1].start()
    angle_g = float(g) * freq * slice_time
    cosg, sing = jnp.cos(angle_g), jnp.sin(angle_g)
    for k in range(1, g):
        grp_arrival(k).wait_recv()

    def tot_copy(k):
        return pltpu.make_async_remote_copy(
            src_ref=tot, dst_ref=carry_in.at[k - 1],
            send_sem=tot_send.at[k - 1], recv_sem=tot_recv.at[k - 1],
            device_id={"tm": ((q + k) % ng) * g + r},
        )

    if ng > 1:
        value = load_planes(grp.at[0])
        for m in range(1, g):
            moved = drift(value, cos1, sin1, freq)
            value = tuple(a + b for a, b in zip(moved, load_planes(grp.at[m])))
        store_planes(tot, value)
        for k in range(1, ng):
            @pl.when(q + k < ng)
            def _(k=k):
                tot_copy(k).start()

    value = tuple(jnp.zeros_like(freq) for _ in range(6))
    for k in range(ng - 1, 0, -1):
        @pl.when(k <= q)
        def _(k=k):
            tot_copy(k).wait_recv()

        here = k <= q
        moved = drift(value, cosg, sing, freq)
        value = tuple(
            jnp.where(here, a + b, c)
            for a, b, c in zip(moved, load_planes(carry_in.at[k - 1]), value)
        )
    for m in range(g - 1):
        here = m < r
        moved = drift(value, cos1, sin1, freq)
        value = tuple(
            jnp.where(here, a + b, c)
            for a, b, c in zip(moved, load_planes(grp.at[m]), value)
        )
    store_planes(next_ref, tuple(jnp.where(first, a, b) for a, b in zip(own, value)))

    leaving[2].start()
    for k in range(1, nb):
        body_copy(0, k, state_ref).wait_send()
        mass_copy(k).wait_send()
        for step in range(2):
            body_copy(step + 1, k, sendbuf.at[step]).wait_send()
    for k in range(1, g):
        grp_copy(k).wait_send()
    for k in range(1, ng):
        @pl.when(q + k < ng)
        def _(k=k):
            tot_copy(k).wait_send()
    for copy in leaving:
        copy.wait()


def solution(mesh):
    nt = mesh.shape["tm"]
    nb = mesh.shape["body"]
    g = group_size(nt)
    ng = nt // g

    def local(states, masses, frequency):
        lanes = states.shape[2]
        s = lanes // 128
        dma = pltpu.SemaphoreType.DMA
        anywhere = pl.BlockSpec(memory_space=pl.ANY)
        outs = pl.pallas_call(
            functools.partial(kernel, nt, nb, g),
            out_shape=jax.ShapeDtypeStruct((3, 6, s, 128), F32),
            in_specs=[anywhere] * 3,
            out_specs=anywhere,
            scratch_shapes=[
                pltpu.VMEM((6, s, 128), F32),
                pltpu.VMEM((s, 128), F32),
                pltpu.VMEM((s, 128), F32),
                pltpu.VMEM((6, s, 128), F32),
                pltpu.VMEM((6, s, 128), F32),
                pltpu.VMEM((6, s, 128), F32),
                pltpu.VMEM((4, s, FEATURES, 128), F32),
                pltpu.VMEM((nb, lanes, FEATURES), BF16),
                pltpu.VMEM((nb, SUM_ROWS, lanes), BF16),
                pltpu.VMEM((FEATURES, lanes), BF16),
                pltpu.VMEM((FEATURES, lanes), BF16),
                pltpu.VMEM((s, HALF_ROWS, 128), F32),
                pltpu.VMEM((s, HALF_ROWS, 128), F32),
                pltpu.VMEM((2, 6, s, 128), F32),
                pltpu.VMEM((3, max(nb - 1, 1), 6, s, 128), F32),
                pltpu.VMEM((max(nb - 1, 1), s, 128), F32),
                pltpu.VMEM((g, 6, s, 128), F32),
                pltpu.VMEM((6, s, 128), F32),
                pltpu.VMEM((max(ng - 1, 1), 6, s, 128), F32),
                dma((3,)),
                dma((3,)),
                dma((3, max(nb - 1, 1))),
                dma((3, max(nb - 1, 1))),
                dma((max(nb - 1, 1),)),
                dma((max(nb - 1, 1),)),
                dma((max(g - 1, 1),)),
                dma((g,)),
                dma((max(ng - 1, 1),)),
                dma((max(ng - 1, 1),)),
                pltpu.SemaphoreType.REGULAR((2,)),
            ],
            compiler_params=pltpu.CompilerParams(
                collective_id=0, has_side_effects=True
            ),
        )(
            states.reshape(6, s, 128),
            masses.reshape(s, 128),
            frequency.reshape(s, 128),
        )
        return tuple(outs[n].reshape(1, 6, lanes) for n in range(3))

    placed = (P("tm", None, "body"), P("body"), P("body"))
    return jax.shard_map(
        local,
        mesh=mesh,
        in_specs=placed,
        out_specs=(P("tm", None, "body"),) * 3,
        check_vma=False,
    )
```

```python
import functools

import jax
import jax.numpy as jnp
from jax import lax
from jax.experimental import pallas as pl
from jax.experimental.pallas import tpu as pltpu
from jax.sharding import PartitionSpec as P

slice_time = 0.25
fine_step = 0.125
soften_sq = 0.01
disc_mass = 1.0

F32 = jnp.float32
BF16 = jnp.bfloat16
FEATURES = 48
SUM_ROWS = 16
HALF_ROWS = 8
TILE_I = 256


def group_size(count):
    best = 1
    for size in range(1, count + 1):
        if count % size == 0 and size * size <= count:
            best = size
    return best


def split3(value):
    high = value.astype(BF16).astype(F32)
    rest = value - high
    middle = rest.astype(BF16).astype(F32)
    return high, middle, rest - middle


def split2(value):
    high = value.astype(BF16).astype(F32)
    return high, value - high


def drift(planes, cos_turn, sin_turn, frequency):
    x, y, z, vx, vy, vz = planes
    return (
        cos_turn * x - sin_turn * y,
        sin_turn * x + cos_turn * y,
        cos_turn * z + sin_turn * vz / frequency,
        cos_turn * vx - sin_turn * vy,
        sin_turn * vx + cos_turn * vy,
        cos_turn * vz - sin_turn * frequency * z,
    )


def load_planes(ref):
    return tuple(ref[c] for c in range(6))


def store_planes(ref, planes):
    for c in range(6):
        ref[c] = planes[c]


def plane_sum(planes_a, planes_b):
    return sum(a * b for a, b in zip(planes_a, planes_b))


def kernel(
    nt, nb, g,
    state_hbm, mass_hbm, freq_hbm,
    out_ref,
    state_ref, mass_ref, freq_ref,
    lhs, weigh, rhs_r, rhs_c, sum_s, sum_t,
    rows, got, got_mass, grp, tot, carry_in,
    in_sem,
    body_send, body_recv, mass_send, mass_recv,
    grp_send, grp_recv, tot_send, tot_recv, entered,
):
    slot = lax.axis_index("tm")
    half = lax.axis_index("body")
    ng = nt // g
    q = slot // g
    r = slot % g
    chunks = state_ref.shape[1]
    lanes = chunks * 128
    wide = TILE_I // 128 if chunks % (TILE_I // 128) == 0 else 1
    span = wide * 128
    touched = set()
    mass_scale = disc_mass / (lanes * nb)

    barrier = pltpu.get_barrier_semaphore()
    split = nb == 2
    later_peers = (g - 1) + (ng - 1)

    def greet_slices():
        for k in range(1, g):
            pl.semaphore_signal(barrier, inc=1, device_id={"tm": q * g + (r + k) % g})
        for k in range(1, ng):
            pl.semaphore_signal(
                barrier, inc=1, device_id={"tm": ((q + k) % ng) * g + r}
            )

    def greet():
        if split:
            @pl.when(half == 1)
            def _():
                pl.semaphore_signal(barrier, inc=1, device_id={"body": 1 - half})
        else:
            for k in range(1, nb):
                pl.semaphore_signal(barrier, inc=1, device_id={"body": (half + k) % nb})
            greet_slices()

    def meet_partner():
        if split:
            @pl.when(half == 0)
            def _():
                pl.semaphore_wait(barrier, 1)
                pl.semaphore_signal(entered.at[0], inc=1, device_id={"body": 1 - half})

            @pl.when(half == 1)
            def _():
                pl.semaphore_wait(entered.at[0], 1)
                greet_slices()
        else:
            pl.semaphore_wait(barrier, (nb - 1) + later_peers)

    def meet_slices():
        if split and later_peers:
            @pl.when(half == 1)
            def _():
                pl.semaphore_wait(barrier, later_peers)
                pl.semaphore_signal(entered.at[1], inc=1, device_id={"body": 1 - half})

            @pl.when(half == 0)
            def _():
                pl.semaphore_wait(entered.at[1], 1)

    greet()
    arrivals = [
        pltpu.make_async_copy(src, dst, in_sem.at[n])
        for n, (src, dst) in enumerate(
            ((state_hbm, state_ref), (mass_hbm, mass_ref), (freq_hbm, freq_ref))
        )
    ]
    for copy in arrivals:
        copy.start()

    def body_copy(turn, k):
        return pltpu.make_async_remote_copy(
            src_ref=rows.at[turn], dst_ref=got.at[turn, k - 1],
            send_sem=body_send.at[turn, k - 1], recv_sem=body_recv.at[turn, k - 1],
            device_id={"body": (half + k) % nb},
        )

    def mass_copy(k):
        return pltpu.make_async_remote_copy(
            src_ref=mass_ref, dst_ref=got_mass.at[k - 1],
            send_sem=mass_send.at[k - 1], recv_sem=mass_recv.at[k - 1],
            device_id={"body": (half + k) % nb},
        )

    row = lax.broadcasted_iota(jnp.int32, (8, 128), 0)
    norm_row, closing_row = row == 3, row == 7
    free_row = norm_row | closing_row
    to_dist = jnp.where(row < 3, -2.0, jnp.where(norm_row, 1.0, 0.0))
    soften = jnp.where(norm_row, soften_sq, 0.0)
    to_closing = jnp.where(norm_row, 1.0, jnp.where(closing_row, 0.0, -1.0))

    def publish(turn, planes):
        places, speeds = planes[:3], planes[3:]
        order = places + (plane_sum(places, places),)
        order = order + speeds + (plane_sum(places, speeds),)
        for c in range(8):
            rows[turn, :, c, :] = order[c]

    def prepare_source(block, ref, mass):
        for s in range(chunks):
            body = ref[s]
            high, middle, low = split3(body)
            first = jnp.where(free_row, 1.0, high)
            second = jnp.where(free_row, 1.0, middle)
            feature = jnp.concatenate([high, first, first, middle, second, low], axis=0)
            lhs[block, s * 128 : (s + 1) * 128, :] = feature.astype(BF16).T
            weight = jnp.broadcast_to(mass[s : s + 1, :], (8, 128)) * mass_scale
            heavy = jnp.where(closing_row, 0.0, weight * body)
            heavy = split2(jnp.where(norm_row, weight, heavy))
            weigh[block, :, s * 128 : (s + 1) * 128] = jnp.concatenate(
                heavy, axis=0
            ).astype(BF16)

    def prepare_target(ref):
        for s in range(chunks):
            body = ref[s]
            high, middle, low = split3(to_dist * body + soften)
            one = jnp.where(norm_row, 1.0, high)
            cross = jnp.where(norm_row, high, middle)
            rhs_r[:, s * 128 : (s + 1) * 128] = jnp.concatenate(
                [one, middle, low, one, cross, one], axis=0
            ).astype(BF16)
            high, middle, low = split3(to_closing * pltpu.roll(body, 4, 0))
            one = jnp.where(free_row, jnp.where(norm_row, 0.0, 1.0), high)
            cross = jnp.where(norm_row, high, middle)
            rhs_c[:, s * 128 : (s + 1) * 128] = jnp.concatenate(
                [one, middle, low, one, cross, one], axis=0
            ).astype(BF16)

    def visit(tiles):
        def pair(tile):
            block, at, n = tile
            rows = lhs[block, at * span : (at + 1) * span, :]
            cols = slice(n * span, (n + 1) * span)
            dist = jnp.dot(rows, rhs_r[:, cols], preferred_element_type=F32)
            closing = jnp.dot(rows, rhs_c[:, cols], preferred_element_type=F32)
            return dist, closing

        def curve(dist, closing):
            inverse = lax.rsqrt(dist)
            square = inverse * inverse
            strength = square * inverse
            turning = (closing * square) * strength
            s_high = strength.astype(BF16)
            s_low = (strength - s_high.astype(F32)).astype(BF16)
            return s_high, s_low, turning.astype(BF16)

        def collect(block, at, n, parts, dims):
            weights = weigh[block, :, at * span : (at + 1) * span]
            new = [
                lax.dot_general(weights, part, (dims, ((), ())), preferred_element_type=F32)
                for part in parts
            ]
            new_s, new_t = (
                a[:HALF_ROWS] + a[HALF_ROWS:] for a in (new[0] + new[1], new[2])
            )
            fresh = n not in touched
            touched.add(n)
            for m in range(wide):
                piece = slice(m * 128, (m + 1) * 128)
                if fresh:
                    sum_s[n * wide + m] = new_s[:, piece]
                    sum_t[n * wide + m] = new_t[:, piece]
                else:
                    sum_s[n * wide + m] += new_s[:, piece]
                    sum_t[n * wide + m] += new_t[:, piece]

        def gather(tile, parts):
            block, at, n = tile
            collect(block, at, n, parts, ((1,), (0,)))
            if block == 0 and at != n:
                collect(block, n, at, parts, ((1,), (1,)))

        ready, parts = pair(tiles[0]), None
        for index in range(len(tiles)):
            now = ready
            if index + 1 < len(tiles):
                ready = pair(tiles[index + 1])
            if index > 0:
                gather(tiles[index - 1], parts)
            parts = curve(*now)
        gather(tiles[-1], parts)

    def forces(turn, planes):
        publish(turn, planes)
        if turn == 0:
            meet_partner()
        for k in range(1, nb):
            body_copy(turn, k).start()
            if turn == 0:
                mass_copy(k).start()
        prepare_source(0, rows.at[turn], mass_ref)
        prepare_target(rows.at[turn])
        touched.clear()
        squares = range(chunks // wide)
        visit([(0, at, n) for n in squares for at in squares if at >= n])
        for k in range(1, nb):
            body_copy(turn, k).wait_recv()
            if turn == 0:
                mass_copy(k).wait_recv()
            prepare_source(k, got.at[turn, k - 1], got_mass.at[k - 1])
            visit([(k, at, n) for n in squares for at in squares])

        def summed(ref, c):
            return ref[:, c, :]

        places, speeds = planes[:3], planes[3:]
        total, turned = summed(sum_s, 3), summed(sum_t, 3)
        inverse = lax.rsqrt(plane_sum(places, places))
        cube = inverse * inverse * inverse
        pull = 3.0 * plane_sum(places, speeds) * inverse * inverse
        acc, jerk = [], []
        for c in range(3):
            p, v = places[c], speeds[c]
            acc.append(summed(sum_s, c) - p * total - cube * p)
            spin = summed(sum_s, 4 + c) - v * total
            spin = spin - 3.0 * (summed(sum_t, c) - p * turned)
            jerk.append(spin - cube * (v - pull * p))
        return acc, jerk

    for copy in arrivals:
        copy.wait()
    planes = load_planes(state_ref)
    h = fine_step
    acc, jerk = forces(0, planes)
    for step in range(2):
        pos, vel = planes[:3], planes[3:]
        guess = tuple(
            p + h * v + h * h / 2.0 * a + h**3 / 6.0 * j
            for p, v, a, j in zip(pos, vel, acc, jerk)
        ) + tuple(v + h * a + h * h / 2.0 * j for v, a, j in zip(vel, acc, jerk))
        na, nj = forces(step + 1, guess)
        new_vel = tuple(
            vel[c] + h / 2.0 * (acc[c] + na[c]) + h * h / 12.0 * (jerk[c] - nj[c])
            for c in range(3)
        )
        new_pos = tuple(
            pos[c] + h / 2.0 * (vel[c] + new_vel[c]) + h * h / 12.0 * (acc[c] - na[c])
            for c in range(3)
        )
        planes, acc, jerk = new_pos + new_vel, na, nj
        if step == 0:
            meet_slices()

    freq = freq_ref[...]
    angle = freq * slice_time
    cos1, sin1 = jnp.cos(angle), jnp.sin(angle)
    fine = planes
    own = load_planes(state_ref)
    coarse = drift(own, cos1, sin1, freq)
    corr = tuple(a - b for a, b in zip(fine, coarse))
    first = slot == 0
    store_planes(grp.at[r], tuple(jnp.where(first, a, b) for a, b in zip(fine, corr)))
    store_planes(out_ref.at[0], fine)
    store_planes(out_ref.at[1], corr)

    def grp_copy(k):
        return pltpu.make_async_remote_copy(
            src_ref=grp.at[r], dst_ref=grp.at[r],
            send_sem=grp_send.at[k - 1], recv_sem=grp_recv.at[r],
            device_id={"tm": q * g + (r + k) % g},
        )

    def grp_arrival(k):
        source = (r + g - k) % g
        return pltpu.make_async_remote_copy(
            src_ref=grp.at[source], dst_ref=grp.at[source],
            send_sem=grp_send.at[k - 1], recv_sem=grp_recv.at[source],
            device_id={"tm": q * g + (r + k) % g},
        )

    for k in range(1, g):
        grp_copy(k).start()
    angle_g = float(g) * freq * slice_time
    cosg, sing = jnp.cos(angle_g), jnp.sin(angle_g)
    for k in range(1, g):
        grp_arrival(k).wait_recv()

    def tot_copy(k):
        return pltpu.make_async_remote_copy(
            src_ref=tot, dst_ref=carry_in.at[k - 1],
            send_sem=tot_send.at[k - 1], recv_sem=tot_recv.at[k - 1],
            device_id={"tm": ((q + k) % ng) * g + r},
        )

    if ng > 1:
        value = load_planes(grp.at[0])
        for m in range(1, g):
            moved = drift(value, cos1, sin1, freq)
            value = tuple(a + b for a, b in zip(moved, load_planes(grp.at[m])))
        store_planes(tot, value)
        for k in range(1, ng):
            @pl.when(q + k < ng)
            def _(k=k):
                tot_copy(k).start()

    value = tuple(jnp.zeros_like(freq) for _ in range(6))
    for k in range(ng - 1, 0, -1):
        @pl.when(k <= q)
        def _(k=k):
            tot_copy(k).wait_recv()

        here = k <= q
        moved = drift(value, cosg, sing, freq)
        value = tuple(
            jnp.where(here, a + b, c)
            for a, b, c in zip(moved, load_planes(carry_in.at[k - 1]), value)
        )
    for m in range(g - 1):
        here = m < r
        moved = drift(value, cos1, sin1, freq)
        value = tuple(
            jnp.where(here, a + b, c)
            for a, b, c in zip(moved, load_planes(grp.at[m]), value)
        )
    store_planes(out_ref.at[2], tuple(jnp.where(first, a, b) for a, b in zip(own, value)))

    for k in range(1, nb):
        mass_copy(k).wait_send()
        for turn in range(3):
            body_copy(turn, k).wait_send()
    for k in range(1, g):
        grp_copy(k).wait_send()
    for k in range(1, ng):
        @pl.when(q + k < ng)
        def _(k=k):
            tot_copy(k).wait_send()


def solution(mesh):
    nt = mesh.shape["tm"]
    nb = mesh.shape["body"]
    g = group_size(nt)
    ng = nt // g

    def local(states, masses, frequency):
        lanes = states.shape[2]
        s = lanes // 128
        dma = pltpu.SemaphoreType.DMA
        anywhere = pl.BlockSpec(memory_space=pl.ANY)
        outs = pl.pallas_call(
            functools.partial(kernel, nt, nb, g),
            out_shape=pltpu.VMEM((3, 6, s, 128), F32),
            in_specs=[anywhere] * 3,
            out_specs=pl.BlockSpec(memory_space=pltpu.VMEM),
            scratch_shapes=[
                pltpu.VMEM((6, s, 128), F32),
                pltpu.VMEM((s, 128), F32),
                pltpu.VMEM((s, 128), F32),
                pltpu.VMEM((nb, lanes, FEATURES), BF16),
                pltpu.VMEM((nb, SUM_ROWS, lanes), BF16),
                pltpu.VMEM((FEATURES, lanes), BF16),
                pltpu.VMEM((FEATURES, lanes), BF16),
                pltpu.VMEM((s, HALF_ROWS, 128), F32),
                pltpu.VMEM((s, HALF_ROWS, 128), F32),
                pltpu.VMEM((3, s, 8, 128), F32),
                pltpu.VMEM((3, max(nb - 1, 1), s, 8, 128), F32),
                pltpu.VMEM((max(nb - 1, 1), s, 128), F32),
                pltpu.VMEM((g, 6, s, 128), F32),
                pltpu.VMEM((6, s, 128), F32),
                pltpu.VMEM((max(ng - 1, 1), 6, s, 128), F32),
                dma((3,)),
                dma((3, max(nb - 1, 1))),
                dma((3, max(nb - 1, 1))),
                dma((max(nb - 1, 1),)),
                dma((max(nb - 1, 1),)),
                dma((max(g - 1, 1),)),
                dma((g,)),
                dma((max(ng - 1, 1),)),
                dma((max(ng - 1, 1),)),
                pltpu.SemaphoreType.REGULAR((2,)),
            ],
            compiler_params=pltpu.CompilerParams(
                collective_id=0, has_side_effects=True
            ),
        )(
            states.reshape(6, s, 128),
            masses.reshape(s, 128),
            frequency.reshape(s, 128),
        )
        return tuple(outs[n].reshape(1, 6, lanes) for n in range(3))

    placed = (P("tm", None, "body"), P("body"), P("body"))
    return jax.shard_map(
        local,
        mesh=mesh,
        in_specs=placed,
        out_specs=(P("tm", None, "body"),) * 3,
        check_vma=False,
    )
```

```python
import functools

import jax
import jax.numpy as jnp
from jax import lax
from jax.experimental import pallas as pl
from jax.experimental.pallas import tpu as pltpu
from jax.sharding import PartitionSpec as P

slice_time = 0.25
fine_step = 0.125
soften_sq = 0.01
disc_mass = 1.0

F32 = jnp.float32
BF16 = jnp.bfloat16
FEATURES = 48
SUM_ROWS = 16
HALF_ROWS = 8
TILE_I = 256
AHEAD = 1


def group_size(count):
    best = 1
    for size in range(1, count + 1):
        if count % size == 0 and size * size <= count:
            best = size
    return best


def tile_chunks(chunks):
    return TILE_I // 128 if chunks % (TILE_I // 128) == 0 else 1


def split3(value):
    high = value.astype(BF16).astype(F32)
    rest = value - high
    middle = rest.astype(BF16).astype(F32)
    return high, middle, rest - middle


def split2(value):
    high = value.astype(BF16).astype(F32)
    return high, value - high


def drift(planes, cos_turn, sin_turn, frequency):
    x, y, z, vx, vy, vz = planes
    return (
        cos_turn * x - sin_turn * y,
        sin_turn * x + cos_turn * y,
        cos_turn * z + sin_turn * vz / frequency,
        cos_turn * vx - sin_turn * vy,
        sin_turn * vx + cos_turn * vy,
        cos_turn * vz - sin_turn * frequency * z,
    )


def load_planes(ref):
    return tuple(ref[c] for c in range(6))


def store_planes(ref, planes):
    for c in range(6):
        ref[c] = planes[c]


def plane_sum(planes_a, planes_b):
    return sum(a * b for a, b in zip(planes_a, planes_b))


def kernel(
    nt, nb, g,
    state_hbm, mass_hbm, freq_hbm,
    out_ref,
    state_ref, mass_ref, freq_ref,
    lhs, weigh, rhs_r, rhs_c, sum_s, sum_t,
    rows, got, got_mass, own_term, col_in, note, note_in,
    in_sem,
    body_send, body_recv, mass_send, mass_recv,
    col_send, col_recv, note_send, note_recv, entered,
):
    slot = lax.axis_index("tm")
    half = lax.axis_index("body")
    ng = nt // g
    q = slot // g
    r = slot % g
    chunks = state_ref.shape[1]
    lanes = chunks * 128
    wide = tile_chunks(chunks)
    span = wide * 128
    squares = range(chunks // wide)
    touched = set()
    mass_scale = disc_mass / (lanes * nb)

    barrier = pltpu.get_barrier_semaphore()
    split = nb == 2
    later_peers = (g - 1) + (ng - 1)

    def greet_slices():
        for k in range(1, g):
            pl.semaphore_signal(barrier, inc=1, device_id={"tm": q * g + (r + k) % g})
        for k in range(1, ng):
            pl.semaphore_signal(
                barrier, inc=1, device_id={"tm": ((q + k) % ng) * g + r}
            )

    def greet():
        if split:
            @pl.when(half == 1)
            def _():
                pl.semaphore_signal(barrier, inc=1, device_id={"body": 1 - half})
        else:
            for k in range(1, nb):
                pl.semaphore_signal(barrier, inc=1, device_id={"body": (half + k) % nb})
            greet_slices()

    def meet_partner():
        if split:
            @pl.when(half == 0)
            def _():
                pl.semaphore_wait(barrier, 1)
                pl.semaphore_signal(entered.at[0], inc=1, device_id={"body": 1 - half})

            @pl.when(half == 1)
            def _():
                pl.semaphore_wait(entered.at[0], 1)
                greet_slices()
        else:
            pl.semaphore_wait(barrier, (nb - 1) + later_peers)

    def meet_slices():
        if split and later_peers:
            @pl.when(half == 1)
            def _():
                pl.semaphore_wait(barrier, later_peers)
                pl.semaphore_signal(entered.at[1], inc=1, device_id={"body": 1 - half})

            @pl.when(half == 0)
            def _():
                pl.semaphore_wait(entered.at[1], 1)

    greet()
    arrivals = [
        pltpu.make_async_copy(src, dst, in_sem.at[n])
        for n, (src, dst) in enumerate(
            ((state_hbm, state_ref), (mass_hbm, mass_ref), (freq_hbm, freq_ref))
        )
    ]
    for copy in arrivals:
        copy.start()

    def body_copy(turn, k):
        return pltpu.make_async_remote_copy(
            src_ref=rows.at[turn], dst_ref=got.at[turn, k - 1],
            send_sem=body_send.at[turn, k - 1], recv_sem=body_recv.at[turn, k - 1],
            device_id={"body": (half + k) % nb},
        )

    def mass_copy(k):
        return pltpu.make_async_remote_copy(
            src_ref=mass_ref, dst_ref=got_mass.at[k - 1],
            send_sem=mass_send.at[k - 1], recv_sem=mass_recv.at[k - 1],
            device_id={"body": (half + k) % nb},
        )

    row = lax.broadcasted_iota(jnp.int32, (8, 128), 0)
    norm_row, closing_row = row == 3, row == 7
    free_row = norm_row | closing_row
    to_dist = jnp.where(row < 3, -2.0, jnp.where(norm_row, 1.0, 0.0))
    soften = jnp.where(norm_row, soften_sq, 0.0)
    to_closing = jnp.where(norm_row, 1.0, jnp.where(closing_row, 0.0, -1.0))

    def publish(turn, planes):
        places, speeds = planes[:3], planes[3:]
        order = places + (plane_sum(places, places),)
        order = order + speeds + (plane_sum(places, speeds),)
        for c in range(8):
            rows[turn, :, c, :] = order[c]

    def prepare_source(block, ref, mass, square):
        for s in range(square * wide, (square + 1) * wide):
            body = ref[s]
            high, middle, low = split3(body)
            first = jnp.where(free_row, 1.0, high)
            second = jnp.where(free_row, 1.0, middle)
            feature = jnp.concatenate([high, first, first, middle, second, low], axis=0)
            lhs[block, s * 128 : (s + 1) * 128, :] = feature.astype(BF16).T
            weight = jnp.broadcast_to(mass[s : s + 1, :], (8, 128)) * mass_scale
            heavy = jnp.where(closing_row, 0.0, weight * body)
            heavy = split2(jnp.where(norm_row, weight, heavy))
            weigh[block, :, s * 128 : (s + 1) * 128] = jnp.concatenate(
                heavy, axis=0
            ).astype(BF16)

    def prepare_target(ref, square):
        for s in range(square * wide, (square + 1) * wide):
            body = ref[s]
            high, middle, low = split3(to_dist * body + soften)
            one = jnp.where(norm_row, 1.0, high)
            cross = jnp.where(norm_row, high, middle)
            rhs_r[:, s * 128 : (s + 1) * 128] = jnp.concatenate(
                [one, middle, low, one, cross, one], axis=0
            ).astype(BF16)
            high, middle, low = split3(to_closing * pltpu.roll(body, 4, 0))
            one = jnp.where(free_row, jnp.where(norm_row, 0.0, 1.0), high)
            cross = jnp.where(norm_row, high, middle)
            rhs_c[:, s * 128 : (s + 1) * 128] = jnp.concatenate(
                [one, middle, low, one, cross, one], axis=0
            ).astype(BF16)

    def visit(turn, tiles, done):
        built = set()

        def build(tile):
            block, at, n = tile
            if block > 0 and (block,) not in built:
                body_copy(turn, block).wait_recv()
                if turn == 0:
                    mass_copy(block).wait_recv()
            if (block, at) not in built:
                if block == 0:
                    prepare_source(0, rows.at[turn], mass_ref, at)
                else:
                    prepare_source(
                        block, got.at[turn, block - 1], got_mass.at[block - 1], at
                    )
            if ("target", n) not in built:
                prepare_target(rows.at[turn], n)
            built.update([(block,), (block, at), ("target", n)])

        def pair(tile):
            block, at, n = tile
            source = lhs[block, at * span : (at + 1) * span, :]
            cols = slice(n * span, (n + 1) * span)
            dist = jnp.dot(source, rhs_r[:, cols], preferred_element_type=F32)
            closing = jnp.dot(source, rhs_c[:, cols], preferred_element_type=F32)
            return dist, closing

        def curve(dist, closing):
            inverse = lax.rsqrt(dist)
            square = inverse * inverse
            strength = square * inverse
            turning = (closing * square) * strength
            s_high = strength.astype(BF16)
            s_low = (strength - s_high.astype(F32)).astype(BF16)
            return s_high, s_low, turning.astype(BF16)

        def collect(block, at, n, parts, dims):
            weights = weigh[block, :, at * span : (at + 1) * span]
            new = [
                lax.dot_general(weights, part, (dims, ((), ())), preferred_element_type=F32)
                for part in parts
            ]
            new_s, new_t = (
                a[:HALF_ROWS] + a[HALF_ROWS:] for a in (new[0] + new[1], new[2])
            )
            fresh = n not in touched
            touched.add(n)
            for m in range(wide):
                piece = slice(m * 128, (m + 1) * 128)
                if fresh:
                    sum_s[n * wide + m] = new_s[:, piece]
                    sum_t[n * wide + m] = new_t[:, piece]
                else:
                    sum_s[n * wide + m] += new_s[:, piece]
                    sum_t[n * wide + m] += new_t[:, piece]

        def gather(tile, parts):
            block, at, n = tile
            collect(block, at, n, parts, ((1,), (0,)))
            if block == 0 and at != n:
                collect(block, n, at, parts, ((1,), (1,)))

        for tile in tiles[: AHEAD + 1]:
            build(tile)
        ready, parts = pair(tiles[0]), None
        for index, tile in enumerate(tiles):
            now = ready
            if index + AHEAD + 1 < len(tiles):
                build(tiles[index + AHEAD + 1])
            if index + 1 < len(tiles):
                ready = pair(tiles[index + 1])
            if index > 0:
                gather(tiles[index - 1], parts)
                done(index - 1)
            parts = curve(*now)
        gather(tiles[-1], parts)
        done(len(tiles) - 1)

    def pulls(planes):
        places, speeds = planes[:3], planes[3:]
        total, turned = sum_s[:, 3, :], sum_t[:, 3, :]
        inverse = lax.rsqrt(plane_sum(places, places))
        cube = inverse * inverse * inverse
        pull = 3.0 * plane_sum(places, speeds) * inverse * inverse
        acc, jerk = [], []
        for c in range(3):
            p, v = places[c], speeds[c]
            acc.append(sum_s[:, c, :] - p * total - cube * p)
            spin = sum_s[:, 4 + c, :] - v * total
            spin = spin - 3.0 * (sum_t[:, c, :] - p * turned)
            jerk.append(spin - cube * (v - pull * p))
        return acc, jerk

    def visits(turn, planes, done):
        publish(turn, planes)
        if turn == 0:
            meet_partner()
        for k in range(1, nb):
            body_copy(turn, k).start()
            if turn == 0:
                mass_copy(k).start()
        touched.clear()
        visit(turn, tiles, done)

    def forces(turn, planes):
        visits(turn, planes, lambda index: None)
        return pulls(planes)

    tiles = [(0, at, n) for n in squares for at in squares if at >= n]
    tiles += [(k, at, n) for k in range(1, nb) for n in squares for at in squares]

    for copy in arrivals:
        copy.wait()
    planes = load_planes(state_ref)
    h = fine_step
    freq = freq_ref[...]
    angle = freq * slice_time
    cos1, sin1 = jnp.cos(angle), jnp.sin(angle)
    angle_g = float(g) * freq * slice_time
    cosg, sing = jnp.cos(angle_g), jnp.sin(angle_g)
    own = planes
    coarse = drift(own, cos1, sin1, freq)
    first = slot == 0

    def predict(planes, acc, jerk):
        pos, vel = planes[:3], planes[3:]
        return tuple(
            p + h * v + h * h / 2.0 * a + h**3 / 6.0 * j
            for p, v, a, j in zip(pos, vel, acc, jerk)
        ) + tuple(v + h * a + h * h / 2.0 * j for v, a, j in zip(vel, acc, jerk))

    def correct(planes, acc, jerk, na, nj):
        pos, vel = planes[:3], planes[3:]
        new_vel = tuple(
            vel[c] + h / 2.0 * (acc[c] + na[c]) + h * h / 12.0 * (jerk[c] - nj[c])
            for c in range(3)
        )
        new_pos = tuple(
            pos[c] + h / 2.0 * (vel[c] + new_vel[c]) + h * h / 12.0 * (acc[c] - na[c])
            for c in range(3)
        )
        return new_pos + new_vel

    acc, jerk = forces(0, planes)
    guess = predict(planes, acc, jerk)
    na, nj = forces(1, guess)
    planes, acc, jerk = correct(planes, acc, jerk, na, nj), na, nj
    meet_slices()
    guess = predict(planes, acc, jerk)

    def col_copy(part, k):
        return pltpu.make_async_remote_copy(
            src_ref=own_term.at[part, :, spans[part]],
            dst_ref=col_in.at[part, k - 1, :, spans[part]],
            send_sem=col_send.at[part, k - 1], recv_sem=col_recv.at[part, k - 1],
            device_id={"tm": ((q + k) % ng) * g + r},
        )

    def note_copy(part, k):
        return pltpu.make_async_remote_copy(
            src_ref=note.at[part, k - 1, :, spans[part]],
            dst_ref=note_in.at[part, k - 1, :, spans[part]],
            send_sem=note_send.at[part, k - 1], recv_sem=note_recv.at[part, k - 1],
            device_id={"tm": q * g + (r + g - k) % g},
        )

    parts = [list(squares)[:-2], *([n] for n in list(squares)[-2:])]
    parts = [group for group in parts if group]
    spans = [
        pl.ds(group[0] * wide, len(group) * wide) for group in parts
    ]
    result = {}

    def finish(part):
        na, nj = pulls(guess)
        fine = correct(planes, acc, jerk, na, nj)
        corr = tuple(a - b for a, b in zip(fine, coarse))
        term = tuple(jnp.where(first, a, b) for a, b in zip(fine, corr))
        store_planes(own_term.at[part], term)
        for k in range(1, ng):
            @pl.when(q + k < ng)
            def _(k=k):
                col_copy(part, k).start()

        result["last"] = fine, corr, term

    final = [max(i for i, tile in enumerate(tiles) if tile[2] in group) for group in parts]
    if nb == 1:
        final = [len(tiles) - 1] * len(parts)

    def done(index):
        for part in range(len(parts)):
            if final[part] == index:
                finish(part)

    visits(2, guess, done)
    fine, corr, term = result["last"]
    store_planes(out_ref.at[0], fine)
    store_planes(out_ref.at[1], corr)

    before = []
    for part in range(len(parts)):
        value = tuple(jnp.zeros_like(freq) for _ in range(6))
        for k in range(ng - 1, 0, -1):
            @pl.when(k <= q)
            def _(k=k):
                col_copy(part, k).wait_recv()

            here = k <= q
            moved = drift(value, cosg, sing, freq)
            value = tuple(
                jnp.where(here, a + b, c)
                for a, b, c in zip(moved, load_planes(col_in.at[part, k - 1]), value)
            )
        before.append(value)
        moved = drift(value, cosg, sing, freq)
        after = tuple(a + b for a, b in zip(moved, term))
        for k in range(1, g):
            up = r >= k
            store_planes(
                note.at[part, k - 1],
                tuple(jnp.where(up, a, b) for a, b in zip(value, after)),
            )

            @pl.when((r < k) | (q > 0))
            def _(k=k):
                note_copy(part, k).start()

    ahead = own
    place = lax.broadcasted_iota(jnp.int32, freq.shape, 0)
    for part in range(len(parts)):
        value = before[part]
        for k in range(1, g):
            here = (r + k >= g) | (q > 0)

            @pl.when(here)
            def _(k=k):
                note_copy(part, k).wait_recv()

            moved = drift(value, cos1, sin1, freq)
            value = tuple(
                jnp.where(here, a + b, a)
                for a, b in zip(moved, load_planes(note_in.at[part, k - 1]))
            )
        low = parts[part][0] * wide
        inside = (place >= low) & (place < low + len(parts[part]) * wide)
        inside = inside & jnp.logical_not(first)
        ahead = tuple(jnp.where(inside, a, b) for a, b in zip(value, ahead))
    store_planes(out_ref.at[2], ahead)

    for k in range(1, nb):
        mass_copy(k).wait_send()
        for turn in range(3):
            body_copy(turn, k).wait_send()
    for part in range(len(parts)):
        for k in range(1, ng):
            @pl.when(q + k < ng)
            def _(k=k):
                col_copy(part, k).wait_send()

        for k in range(1, g):
            @pl.when((r < k) | (q > 0))
            def _(k=k):
                note_copy(part, k).wait_send()


def solution(mesh):
    nt = mesh.shape["tm"]
    nb = mesh.shape["body"]
    g = group_size(nt)
    ng = nt // g

    def local(states, masses, frequency):
        lanes = states.shape[2]
        s = lanes // 128
        wide = tile_chunks(s)
        tiles = s // wide
        dma = pltpu.SemaphoreType.DMA
        anywhere = pl.BlockSpec(memory_space=pl.ANY)
        outs = pl.pallas_call(
            functools.partial(kernel, nt, nb, g),
            out_shape=pltpu.VMEM((3, 6, s, 128), F32),
            in_specs=[anywhere] * 3,
            out_specs=pl.BlockSpec(memory_space=pltpu.VMEM),
            scratch_shapes=[
                pltpu.VMEM((6, s, 128), F32),
                pltpu.VMEM((s, 128), F32),
                pltpu.VMEM((s, 128), F32),
                pltpu.VMEM((nb, lanes, FEATURES), BF16),
                pltpu.VMEM((nb, SUM_ROWS, lanes), BF16),
                pltpu.VMEM((FEATURES, lanes), BF16),
                pltpu.VMEM((FEATURES, lanes), BF16),
                pltpu.VMEM((s, HALF_ROWS, 128), F32),
                pltpu.VMEM((s, HALF_ROWS, 128), F32),
                pltpu.VMEM((3, s, 8, 128), F32),
                pltpu.VMEM((3, max(nb - 1, 1), s, 8, 128), F32),
                pltpu.VMEM((max(nb - 1, 1), s, 128), F32),
                pltpu.VMEM((tiles, 6, s, 128), F32),
                pltpu.VMEM((tiles, max(ng - 1, 1), 6, s, 128), F32),
                pltpu.VMEM((tiles, max(g - 1, 1), 6, s, 128), F32),
                pltpu.VMEM((tiles, max(g - 1, 1), 6, s, 128), F32),
                dma((3,)),
                dma((3, max(nb - 1, 1))),
                dma((3, max(nb - 1, 1))),
                dma((max(nb - 1, 1),)),
                dma((max(nb - 1, 1),)),
                dma((tiles, max(ng - 1, 1))),
                dma((tiles, max(ng - 1, 1))),
                dma((tiles, max(g - 1, 1))),
                dma((tiles, max(g - 1, 1))),
                pltpu.SemaphoreType.REGULAR((2,)),
            ],
            compiler_params=pltpu.CompilerParams(
                collective_id=0, has_side_effects=True
            ),
        )(
            states.reshape(6, s, 128),
            masses.reshape(s, 128),
            frequency.reshape(s, 128),
        )
        return tuple(outs[n].reshape(1, 6, lanes) for n in range(3))

    placed = (P("tm", None, "body"), P("body"), P("body"))
    return jax.shard_map(
        local,
        mesh=mesh,
        in_specs=placed,
        out_specs=(P("tm", None, "body"),) * 3,
        check_vma=False,
    )
```

```python
import functools

import jax
import jax.numpy as jnp
from jax import lax
from jax.experimental import pallas as pl
from jax.experimental.pallas import tpu as pltpu
from jax.sharding import PartitionSpec as P

slice_time = 0.25
fine_step = 0.125
soften_sq = 0.01
disc_mass = 1.0

F32 = jnp.float32
BF16 = jnp.bfloat16
FEATURES = 48
SUM_ROWS = 16
HALF_ROWS = 8
TILE_I = 256
AHEAD = 1


def group_size(count):
    best = 1
    for size in range(1, count + 1):
        if count % size == 0 and size * size <= count:
            best = size
    return best


def tile_chunks(chunks):
    return TILE_I // 128 if chunks % (TILE_I // 128) == 0 else 1


def split3(value):
    high = value.astype(BF16).astype(F32)
    rest = value - high
    middle = rest.astype(BF16).astype(F32)
    return high, middle, rest - middle


def split2(value):
    high = value.astype(BF16).astype(F32)
    return high, value - high


def drift(planes, cos_turn, sin_turn, frequency):
    x, y, z, vx, vy, vz = planes
    return (
        cos_turn * x - sin_turn * y,
        sin_turn * x + cos_turn * y,
        cos_turn * z + sin_turn * vz / frequency,
        cos_turn * vx - sin_turn * vy,
        sin_turn * vx + cos_turn * vy,
        cos_turn * vz - sin_turn * frequency * z,
    )


def load_planes(ref):
    return tuple(ref[c] for c in range(6))


def store_planes(ref, planes):
    for c in range(6):
        ref[c] = planes[c]


def plane_sum(planes_a, planes_b):
    return sum(a * b for a, b in zip(planes_a, planes_b))


def kernel(
    nt, nb, g,
    state_hbm, mass_hbm, freq_hbm,
    out_ref,
    state_ref, mass_ref, freq_ref,
    lhs, weigh, rhs_r, rhs_c, sum_s, sum_t,
    rows, got, got_mass, own_term, col_in, note, note_in,
    in_sem,
    body_send, body_recv, mass_send, mass_recv,
    col_send, col_recv, note_send, note_recv, entered,
):
    slot = lax.axis_index("tm")
    half = lax.axis_index("body")
    ng = nt // g
    q = slot // g
    r = slot % g
    chunks = state_ref.shape[1]
    lanes = chunks * 128
    wide = tile_chunks(chunks)
    span = wide * 128
    squares = range(chunks // wide)
    touched = set()
    mass_scale = disc_mass / (lanes * nb)

    barrier = pltpu.get_barrier_semaphore()
    split = nb == 2
    later_peers = (g - 1) + (ng - 1)

    def greet_slices():
        for k in range(1, g):
            pl.semaphore_signal(barrier, inc=1, device_id={"tm": q * g + (r + k) % g})
        for k in range(1, ng):
            pl.semaphore_signal(
                barrier, inc=1, device_id={"tm": ((q + k) % ng) * g + r}
            )

    def greet():
        if split:
            @pl.when(half == 1)
            def _():
                pl.semaphore_signal(barrier, inc=1, device_id={"body": 1 - half})
        else:
            for k in range(1, nb):
                pl.semaphore_signal(barrier, inc=1, device_id={"body": (half + k) % nb})
            greet_slices()

    def meet_partner():
        if split:
            @pl.when(half == 0)
            def _():
                pl.semaphore_wait(barrier, 1)
                pl.semaphore_signal(entered.at[0], inc=1, device_id={"body": 1 - half})

            @pl.when(half == 1)
            def _():
                pl.semaphore_wait(entered.at[0], 1)
                greet_slices()
        else:
            pl.semaphore_wait(barrier, (nb - 1) + later_peers)

    def meet_slices():
        if split and later_peers:
            @pl.when(half == 1)
            def _():
                pl.semaphore_wait(barrier, later_peers)
                pl.semaphore_signal(entered.at[1], inc=1, device_id={"body": 1 - half})

            @pl.when(half == 0)
            def _():
                pl.semaphore_wait(entered.at[1], 1)

    greet()
    arrivals = [
        pltpu.make_async_copy(src, dst, in_sem.at[n])
        for n, (src, dst) in enumerate(
            ((state_hbm, state_ref), (mass_hbm, mass_ref), (freq_hbm, freq_ref))
        )
    ]
    for copy in arrivals:
        copy.start()

    def body_copy(turn, k):
        return pltpu.make_async_remote_copy(
            src_ref=rows.at[turn], dst_ref=got.at[turn, k - 1],
            send_sem=body_send.at[turn, k - 1], recv_sem=body_recv.at[turn, k - 1],
            device_id={"body": (half + k) % nb},
        )

    def mass_copy(k):
        return pltpu.make_async_remote_copy(
            src_ref=mass_ref, dst_ref=got_mass.at[k - 1],
            send_sem=mass_send.at[k - 1], recv_sem=mass_recv.at[k - 1],
            device_id={"body": (half + k) % nb},
        )

    row = lax.broadcasted_iota(jnp.int32, (8, 128), 0)
    norm_row, closing_row = row == 3, row == 7
    free_row = norm_row | closing_row
    to_dist = jnp.where(row < 3, -2.0, jnp.where(norm_row, 1.0, 0.0))
    soften = jnp.where(norm_row, soften_sq, 0.0)
    to_closing = jnp.where(norm_row, 1.0, jnp.where(closing_row, 0.0, -1.0))

    def publish(turn, planes):
        places, speeds = planes[:3], planes[3:]
        order = places + (plane_sum(places, places),)
        order = order + speeds + (plane_sum(places, speeds),)
        for c in range(8):
            rows[turn, :, c, :] = order[c]

    def prepare_source(block, ref, mass, square):
        for s in range(square * wide, (square + 1) * wide):
            body = ref[s]
            high, middle, low = split3(body)
            first = jnp.where(free_row, 1.0, high)
            second = jnp.where(free_row, 1.0, middle)
            feature = jnp.concatenate([high, first, first, middle, second, low], axis=0)
            lhs[block, s * 128 : (s + 1) * 128, :] = feature.astype(BF16).T
            weight = jnp.broadcast_to(mass[s : s + 1, :], (8, 128)) * mass_scale
            heavy = jnp.where(closing_row, 0.0, weight * body)
            heavy = split2(jnp.where(norm_row, weight, heavy))
            weigh[block, :, s * 128 : (s + 1) * 128] = jnp.concatenate(
                heavy, axis=0
            ).astype(BF16)

    def prepare_target(ref, square):
        for s in range(square * wide, (square + 1) * wide):
            body = ref[s]
            high, middle, low = split3(to_dist * body + soften)
            one = jnp.where(norm_row, 1.0, high)
            cross = jnp.where(norm_row, high, middle)
            rhs_r[:, s * 128 : (s + 1) * 128] = jnp.concatenate(
                [one, middle, low, one, cross, one], axis=0
            ).astype(BF16)
            high, middle, low = split3(to_closing * pltpu.roll(body, 4, 0))
            one = jnp.where(free_row, jnp.where(norm_row, 0.0, 1.0), high)
            cross = jnp.where(norm_row, high, middle)
            rhs_c[:, s * 128 : (s + 1) * 128] = jnp.concatenate(
                [one, middle, low, one, cross, one], axis=0
            ).astype(BF16)

    def visit(turn, tiles, done):
        built = set()

        def build(tile):
            block, at, n = tile
            if block > 0 and (block,) not in built:
                body_copy(turn, block).wait_recv()
                if turn == 0:
                    mass_copy(block).wait_recv()
            if (block, at) not in built:
                if block == 0:
                    prepare_source(0, rows.at[turn], mass_ref, at)
                else:
                    prepare_source(
                        block, got.at[turn, block - 1], got_mass.at[block - 1], at
                    )
            if ("target", n) not in built:
                prepare_target(rows.at[turn], n)
            built.update([(block,), (block, at), ("target", n)])

        def pair(tile):
            block, at, n = tile
            source = lhs[block, at * span : (at + 1) * span, :]
            cols = slice(n * span, (n + 1) * span)
            dist = jnp.dot(source, rhs_r[:, cols], preferred_element_type=F32)
            closing = jnp.dot(source, rhs_c[:, cols], preferred_element_type=F32)
            return dist, closing

        def curve(dist, closing):
            inverse = lax.rsqrt(dist)
            square = inverse * inverse
            strength = square * inverse
            turning = (closing * square) * strength
            s_high = strength.astype(BF16)
            s_low = (strength - s_high.astype(F32)).astype(BF16)
            return s_high, s_low, turning.astype(BF16)

        def collect(block, at, n, parts, dims):
            weights = weigh[block, :, at * span : (at + 1) * span]
            new = [
                lax.dot_general(weights, part, (dims, ((), ())), preferred_element_type=F32)
                for part in parts
            ]
            new_s, new_t = (
                a[:HALF_ROWS] + a[HALF_ROWS:] for a in (new[0] + new[1], new[2])
            )
            fresh = n not in touched
            touched.add(n)
            for m in range(wide):
                piece = slice(m * 128, (m + 1) * 128)
                if fresh:
                    sum_s[n * wide + m] = new_s[:, piece]
                    sum_t[n * wide + m] = new_t[:, piece]
                else:
                    sum_s[n * wide + m] += new_s[:, piece]
                    sum_t[n * wide + m] += new_t[:, piece]

        def gather(tile, parts):
            block, at, n = tile
            collect(block, at, n, parts, ((1,), (0,)))
            if block == 0 and at != n:
                collect(block, n, at, parts, ((1,), (1,)))

        for tile in tiles[: AHEAD + 1]:
            build(tile)
        ready, parts = pair(tiles[0]), None
        for index, tile in enumerate(tiles):
            now = ready
            if index + AHEAD + 1 < len(tiles):
                build(tiles[index + AHEAD + 1])
            if index + 1 < len(tiles):
                ready = pair(tiles[index + 1])
            if index > 0:
                gather(tiles[index - 1], parts)
                done(index - 1)
            parts = curve(*now)
        gather(tiles[-1], parts)
        done(len(tiles) - 1)

    def pulls(planes):
        places, speeds = planes[:3], planes[3:]
        total, turned = sum_s[:, 3, :], sum_t[:, 3, :]
        inverse = lax.rsqrt(plane_sum(places, places))
        cube = inverse * inverse * inverse
        pull = 3.0 * plane_sum(places, speeds) * inverse * inverse
        acc, jerk = [], []
        for c in range(3):
            p, v = places[c], speeds[c]
            acc.append(sum_s[:, c, :] - p * total - cube * p)
            spin = sum_s[:, 4 + c, :] - v * total
            spin = spin - 3.0 * (sum_t[:, c, :] - p * turned)
            jerk.append(spin - cube * (v - pull * p))
        return acc, jerk

    def visits(turn, planes, done):
        publish(turn, planes)
        if turn == 0:
            meet_partner()
        for k in range(1, nb):
            body_copy(turn, k).start()
            if turn == 0:
                mass_copy(k).start()
        touched.clear()
        visit(turn, tiles, done)

    def forces(turn, planes):
        visits(turn, planes, lambda index: None)
        return pulls(planes)

    tiles = [(0, at, n) for n in squares for at in squares if at >= n]
    tiles += [(k, at, n) for k in range(1, nb) for n in squares for at in squares]

    for copy in arrivals:
        copy.wait()
    planes = load_planes(state_ref)
    h = fine_step
    freq = freq_ref[...]
    angle = freq * slice_time
    cos1, sin1 = jnp.cos(angle), jnp.sin(angle)
    angle_g = float(g) * freq * slice_time
    cosg, sing = jnp.cos(angle_g), jnp.sin(angle_g)
    own = planes
    coarse = drift(own, cos1, sin1, freq)
    first = slot == 0

    def predict(planes, acc, jerk):
        pos, vel = planes[:3], planes[3:]
        return tuple(
            p + h * v + h * h / 2.0 * a + h**3 / 6.0 * j
            for p, v, a, j in zip(pos, vel, acc, jerk)
        ) + tuple(v + h * a + h * h / 2.0 * j for v, a, j in zip(vel, acc, jerk))

    def correct(planes, acc, jerk, na, nj):
        pos, vel = planes[:3], planes[3:]
        new_vel = tuple(
            vel[c] + h / 2.0 * (acc[c] + na[c]) + h * h / 12.0 * (jerk[c] - nj[c])
            for c in range(3)
        )
        new_pos = tuple(
            pos[c] + h / 2.0 * (vel[c] + new_vel[c]) + h * h / 12.0 * (acc[c] - na[c])
            for c in range(3)
        )
        return new_pos + new_vel

    acc, jerk = forces(0, planes)
    guess = predict(planes, acc, jerk)
    na, nj = forces(1, guess)
    planes, acc, jerk = correct(planes, acc, jerk, na, nj), na, nj
    meet_slices()
    guess = predict(planes, acc, jerk)

    def col_copy(part, k):
        return pltpu.make_async_remote_copy(
            src_ref=own_term.at[part, :, spans[part]],
            dst_ref=col_in.at[part, k - 1, :, spans[part]],
            send_sem=col_send.at[part, k - 1], recv_sem=col_recv.at[part, k - 1],
            device_id={"tm": ((q + k) % ng) * g + r},
        )

    def note_copy(part, k):
        return pltpu.make_async_remote_copy(
            src_ref=note.at[part, k - 1, :, spans[part]],
            dst_ref=note_in.at[part, k - 1, :, spans[part]],
            send_sem=note_send.at[part, k - 1], recv_sem=note_recv.at[part, k - 1],
            device_id={"tm": q * g + (r + g - k) % g},
        )

    parts = [list(squares)[:-2], *([n] for n in list(squares)[-2:])]
    parts = [group for group in parts if group]
    spans = [
        pl.ds(group[0] * wide, len(group) * wide) for group in parts
    ]
    result = {}

    def finish(part):
        na, nj = pulls(guess)
        fine = correct(planes, acc, jerk, na, nj)
        corr = tuple(a - b for a, b in zip(fine, coarse))
        term = tuple(jnp.where(first, a, b) for a, b in zip(fine, corr))
        store_planes(own_term.at[part], term)
        for k in range(1, ng):
            @pl.when(q + k < ng)
            def _(k=k):
                col_copy(part, k).start()

        result["last"] = fine, corr, term

    final = [max(i for i, tile in enumerate(tiles) if tile[2] in group) for group in parts]
    if nb == 1:
        final = [len(tiles) - 1] * len(parts)

    def done(index):
        for part in range(len(parts)):
            if final[part] == index:
                finish(part)

    visits(2, guess, done)
    fine, corr, term = result["last"]
    store_planes(out_ref.at[0], fine)
    store_planes(out_ref.at[1], corr)

    before = []
    for part in range(len(parts)):
        value = tuple(jnp.zeros_like(freq) for _ in range(6))
        for k in range(ng - 1, 0, -1):
            @pl.when(k <= q)
            def _(k=k):
                col_copy(part, k).wait_recv()

            here = k <= q
            moved = drift(value, cosg, sing, freq)
            value = tuple(
                jnp.where(here, a + b, c)
                for a, b, c in zip(moved, load_planes(col_in.at[part, k - 1]), value)
            )
        before.append(value)
        moved = drift(value, cosg, sing, freq)
        after = tuple(a + b for a, b in zip(moved, term))
        for k in range(g - 1, 0, -1):
            up = r >= k
            store_planes(
                note.at[part, k - 1],
                tuple(jnp.where(up, a, b) for a, b in zip(value, after)),
            )

            @pl.when((r < k) | (q > 0))
            def _(k=k):
                note_copy(part, k).start()

    ahead = own
    place = lax.broadcasted_iota(jnp.int32, freq.shape, 0)
    for part in range(len(parts)):
        value = before[part]
        for k in range(1, g):
            here = (r + k >= g) | (q > 0)

            @pl.when(here)
            def _(k=k):
                note_copy(part, k).wait_recv()

            moved = drift(value, cos1, sin1, freq)
            value = tuple(
                jnp.where(here, a + b, a)
                for a, b in zip(moved, load_planes(note_in.at[part, k - 1]))
            )
        low = parts[part][0] * wide
        inside = (place >= low) & (place < low + len(parts[part]) * wide)
        inside = inside & jnp.logical_not(first)
        ahead = tuple(jnp.where(inside, a, b) for a, b in zip(value, ahead))
    store_planes(out_ref.at[2], ahead)

    for k in range(1, nb):
        mass_copy(k).wait_send()
        for turn in range(3):
            body_copy(turn, k).wait_send()
    for part in range(len(parts)):
        for k in range(1, ng):
            @pl.when(q + k < ng)
            def _(k=k):
                col_copy(part, k).wait_send()

        for k in range(1, g):
            @pl.when((r < k) | (q > 0))
            def _(k=k):
                note_copy(part, k).wait_send()


def solution(mesh):
    nt = mesh.shape["tm"]
    nb = mesh.shape["body"]
    g = group_size(nt)
    ng = nt // g

    def local(states, masses, frequency):
        lanes = states.shape[2]
        s = lanes // 128
        wide = tile_chunks(s)
        tiles = s // wide
        dma = pltpu.SemaphoreType.DMA
        anywhere = pl.BlockSpec(memory_space=pl.ANY)
        outs = pl.pallas_call(
            functools.partial(kernel, nt, nb, g),
            out_shape=pltpu.VMEM((3, 6, s, 128), F32),
            in_specs=[anywhere] * 3,
            out_specs=pl.BlockSpec(memory_space=pltpu.VMEM),
            scratch_shapes=[
                pltpu.VMEM((6, s, 128), F32),
                pltpu.VMEM((s, 128), F32),
                pltpu.VMEM((s, 128), F32),
                pltpu.VMEM((nb, lanes, FEATURES), BF16),
                pltpu.VMEM((nb, SUM_ROWS, lanes), BF16),
                pltpu.VMEM((FEATURES, lanes), BF16),
                pltpu.VMEM((FEATURES, lanes), BF16),
                pltpu.VMEM((s, HALF_ROWS, 128), F32),
                pltpu.VMEM((s, HALF_ROWS, 128), F32),
                pltpu.VMEM((3, s, 8, 128), F32),
                pltpu.VMEM((3, max(nb - 1, 1), s, 8, 128), F32),
                pltpu.VMEM((max(nb - 1, 1), s, 128), F32),
                pltpu.VMEM((tiles, 6, s, 128), F32),
                pltpu.VMEM((tiles, max(ng - 1, 1), 6, s, 128), F32),
                pltpu.VMEM((tiles, max(g - 1, 1), 6, s, 128), F32),
                pltpu.VMEM((tiles, max(g - 1, 1), 6, s, 128), F32),
                dma((3,)),
                dma((3, max(nb - 1, 1))),
                dma((3, max(nb - 1, 1))),
                dma((max(nb - 1, 1),)),
                dma((max(nb - 1, 1),)),
                dma((tiles, max(ng - 1, 1))),
                dma((tiles, max(ng - 1, 1))),
                dma((tiles, max(g - 1, 1))),
                dma((tiles, max(g - 1, 1))),
                pltpu.SemaphoreType.REGULAR((2,)),
            ],
            compiler_params=pltpu.CompilerParams(
                collective_id=0, has_side_effects=True
            ),
        )(
            states.reshape(6, s, 128),
            masses.reshape(s, 128),
            frequency.reshape(s, 128),
        )
        return tuple(outs[n].reshape(1, 6, lanes) for n in range(3))

    placed = (P("tm", None, "body"), P("body"), P("body"))
    return jax.shard_map(
        local,
        mesh=mesh,
        in_specs=placed,
        out_specs=(P("tm", None, "body"),) * 3,
        check_vma=False,
    )
```
